32 devices in a mesh: gx: 4 (over y, x), gy: 8 (over z, core).
Axes of the slice: x: 2, y: 2, z: 4, core: 2. Of those that a mesh axis runs over, the one named last changes fastest.
Arguments:
- links: float32 [4, 3, 3, 2, 8, 16, 6, 128], P(None, None, None, None, 'gx', 'gy'), may hold values from -1 to 1, as said below
- incoming: float32 [4, 3, 3, 2, 8, 16, 4, 128], P(None, None, None, None, 'gx', 'gy'), may hold values from -6 to 6
Outputs:
- force: float32 [4, 3, 3, 2, 8, 16, 4, 128], P(None, None, None, None, 'gx', 'gy')
The draws below stay inside these ranges and needn't reach their ends.
Inputs may be any that keep to these rules, and one draw needn't show every extreme that they name: `links`: each link is a special unitary 3 x 3 matrix.
All inputs are finite; a program needn't handle non-finite values.
Results may differ from the reference program's by a relative error of at most 0.0003.
Values sent between devices are 32-bit elements; how exact they have to be, the bound alone decides.
A program may use at most 128 MiB of HBM per device.

```python
from functools import partial
import jax
import jax.numpy as jnp
from jax import lax

Z = 128
TS = 4
NX = 8
NY = 16


phase_rows = [[0.0, 0.6, -0.6], [0.3, 0.0, -0.3], [0.6, 0.9, -1.5], [0.9, 0.3, -1.2]]


def special_unitary(matrix):
    row_one = matrix[..., 0, :]
    row_one = row_one / jnp.sqrt(jnp.sum(jnp.abs(row_one) ** 2, axis=-1, keepdims=True))
    row_two = matrix[..., 1, :]
    row_two = row_two - jnp.sum(jnp.conj(row_one) * row_two, axis=-1, keepdims=True) * row_one
    row_two = row_two / jnp.sqrt(jnp.sum(jnp.abs(row_two) ** 2, axis=-1, keepdims=True))
    row_three = jnp.conj(jnp.cross(row_one, row_two))
    return jnp.stack([row_one, row_two, row_three], axis=-2)


def matmul_three(former, latter):
    return jnp.einsum('...ij,...jk->...ik', former, latter, precision=lax.Precision.HIGHEST)


def draw_links(key, part):
    gauge_key, noise_key = jax.random.split(jax.random.fold_in(key, 17))
    real_key, imag_key = jax.random.split(gauge_key)
    noise_real_key, noise_imag_key = jax.random.split(noise_key)
    gauge_shape = (NX, NY, TS + 3, Z, 3, 3)
    noise_shape = (4, NX, NY, TS + 2, Z, 3, 3)
    identity = jnp.eye(3, dtype=jnp.float32)
    gauge_real = jax.random.normal(real_key, gauge_shape, jnp.float32)
    gauge_imag = jax.random.normal(imag_key, gauge_shape, jnp.float32)
    noise_real = jax.random.normal(noise_real_key, noise_shape, jnp.float32)
    noise_imag = jax.random.normal(noise_imag_key, noise_shape, jnp.float32)
    gauge = special_unitary(gauge_real + 1j * gauge_imag)
    noise = special_unitary(6.0 * identity + noise_real + 1j * noise_imag)
    coord_x = jnp.arange(NX, dtype=jnp.int32)[:, None, None, None]
    coord_y = jnp.arange(NY, dtype=jnp.int32)[None, :, None, None]
    coord_t = jnp.arange(TS + 2, dtype=jnp.int32)[None, None, :, None]
    coord_z = jnp.arange(Z, dtype=jnp.int32)[None, None, None, :]
    parity = (coord_x + coord_y + coord_t + coord_z) % 2
    sign = 1.0 - 2.0 * parity.astype(jnp.float32)
    table = jnp.array(phase_rows, dtype=jnp.float32)
    angle = table[:, None, None, None, None, :] * sign[None, :, :, :, :, None]
    backbone = jnp.exp(1j * angle)[..., :, None] * identity
    core = matmul_three(backbone, noise)
    here = gauge[:, :, :TS + 2]
    aheads = [jnp.roll(here, -1, axis=0), jnp.roll(here, -1, axis=1), jnp.roll(here, -1, axis=3), gauge[:, :, 1:TS + 3]]
    result = []
    for direction in range(4):
        ahead_dagger = jnp.conj(jnp.swapaxes(aheads[direction], -1, -2))
        result.append(matmul_three(matmul_three(here, core[direction]), ahead_dagger))
    unitary = jnp.stack(result, axis=0)
    stacked = jnp.stack([jnp.real(unitary), jnp.imag(unitary)], axis=-1).astype(jnp.float32)
    return jnp.transpose(stacked, (0, 5, 6, 7, 1, 2, 3, 4))


def shard_levels(rng, shape, cuts, least, largest):
    level, own = 1.0, jax.random.fold_in(rng, 6)
    for position, shards_of in cuts:
        steps = jnp.exp(jax.random.uniform(jax.random.fold_in(own, position), (shards_of,), jnp.float32, least / len(cuts), largest / len(cuts)))
        level = level * jnp.repeat(steps, shape[position] // shards_of).reshape([-1 if axis == position else 1 for axis in range(len(shape))])
    return level


def gaussian(rng, dims, scale, limit, cuts=(), kind=jnp.bfloat16):
    values = scale * jax.random.normal(rng, dims, jnp.float32)
    if cuts:
        values = values * shard_levels(rng, dims, cuts, -0.22, 0.18)
    return jnp.clip(values, -limit, limit).astype(kind)


def setup_inputs(seed: int = 0) -> dict:
    arg_keys = jax.random.split(jax.random.key(seed), 3)
    links = draw_links(jax.random.fold_in(arg_keys[2], 71), 0)
    incoming = gaussian(arg_keys[1], (4, 3, 3, 2, NX, NY, TS, Z), 1.0, 6.0, ((4, 4), (5, 8)), jnp.float32)
    return {"links": links, "incoming": incoming}


smear_weight = 0.2

def product(former, latter):
    former_real, former_imag = former
    latter_real, latter_imag = latter
    real_part = lax.optimization_barrier(jnp.sum(former_real[:, :, None] * latter_real[None] - former_imag[:, :, None] * latter_imag[None], axis=1))
    imag_part = lax.optimization_barrier(jnp.sum(former_real[:, :, None] * latter_imag[None] + former_imag[:, :, None] * latter_real[None], axis=1))
    return (real_part, imag_part)

def adjoint(matrix):
    return (jnp.swapaxes(matrix[0], 0, 1), -jnp.swapaxes(matrix[1], 0, 1))

def summed(former, latter):
    return (former[0] + latter[0], former[1] + latter[1])

def unit_step(which, sign):
    vector = [0, 0, 0, 0]
    vector[which] = sign
    return vector

def offset_list():
    result = [(0, 0, 0, 0)]
    for first in range(4):
        result.append(tuple(unit_step(first, 1)))
        result.append(tuple(unit_step(first, -1)))
        for second in range(4):
            if second != first:
                vector = unit_step(first, 1)
                vector[second] = -1
                result.append(tuple(vector))
    return result

def smeared_term(pieces, incoming, direction):

    def take(which, offset):
        block = pieces[str(tuple(offset))][which]
        return (block[:, :, 0], block[:, :, 1])
    anchor = [0, 0, 0, 0]
    ahead = unit_step(direction, 1)
    own = take(direction, anchor)
    staple = None
    for other in range(4):
        if other == direction:
            continue
        beside = unit_step(other, 1)
        behind = unit_step(other, -1)
        diagonal = [behind[k] + ahead[k] for k in range(4)]
        upper = product(product(take(other, anchor), take(direction, beside)), adjoint(take(other, ahead)))
        lower = product(product(adjoint(take(other, behind)), take(direction, behind)), take(other, diagonal))
        both = summed(upper, lower)
        staple = both if staple is None else summed(staple, both)
    staple = (smear_weight * staple[0], smear_weight * staple[1])
    omega = product(staple, adjoint(own))
    flipped = adjoint(omega)
    anti_real = 0.5 * (omega[0] - flipped[0])
    anti_imag = 0.5 * (omega[1] - flipped[1])
    identity = jnp.eye(3, dtype=jnp.float32)[:, :, None, None, None, None]
    trace_real = anti_real[0, 0] + anti_real[1, 1] + anti_real[2, 2]
    trace_imag = anti_imag[0, 0] + anti_imag[1, 1] + anti_imag[2, 2]
    anti = (anti_real - identity * trace_real / 3.0, anti_imag - identity * trace_imag / 3.0)
    result = (jnp.broadcast_to(identity, anti[0].shape), jnp.zeros_like(anti[1]))
    for order in range(6, 0, -1):
        stepped = product(anti, result)
        result = (identity + stepped[0] / order, stepped[1] / order)
    smeared = product(result, own)
    target = incoming[direction]
    return jnp.sum(target[:, :, 0] * smeared[0] + target[:, :, 1] * smeared[1])

def smear_loss(padded, incoming):
    region_x = padded.shape[4] - 2
    region_y = padded.shape[5] - 2
    slab = incoming.shape[6]
    depth = padded.shape[7]
    wrapped = jnp.concatenate([padded[..., depth - 1:], padded, padded[..., :1]], axis=7)
    pieces = {}
    for offset in offset_list():
        pieces[str(offset)] = wrapped[:, :, :, :, 1 + offset[0]:1 + offset[0] + region_x, 1 + offset[1]:1 + offset[1] + region_y, 1 + offset[3]:1 + offset[3] + slab, 1 + offset[2]:1 + offset[2] + depth]
    total = jnp.float32(0.0)
    for direction in range(4):
        total = total + jax.checkpoint(partial(smeared_term, direction=direction))(pieces, incoming)
    return total

def reference(links, incoming):
    slab = incoming.shape[6]

    def whole_loss(field):
        padded = jnp.pad(field, ((0, 0),) * 4 + ((1, 1), (1, 1)) + ((0, 0), (0, 0)), mode='wrap')
        return smear_loss(padded, incoming)
    grads = jax.grad(whole_loss)(links)
    return grads[:, :, :, :, :, :, 1:1 + slab]
```

```python
from functools import partial

import jax
import jax.numpy as jnp
from jax import lax
from jax.experimental import pallas as pl
from jax.experimental.pallas import tpu as pltpu
from jax.sharding import PartitionSpec as P

smear_weight = 0.2
MESH = pl.DeviceIdType.MESH
AXX, AXY, AXZ, AXT = 0, 1, 2, 3
SENT = 12
COMP = 18
ALG = 8
YSLOT = (1, 0, 2, 3)


def re(i, j):
    return (i * 3 + j) * 2


def cmul(a, b):
    return (a[0] * b[0] - a[1] * b[1], a[0] * b[1] + a[1] * b[0])


def cadd(a, b):
    return (a[0] + b[0], a[1] + b[1])


def conj(a):
    return (a[0], -a[1])


def row_times(row, mat, adj=False, acc=None):
    out = []
    for k in range(3):
        total_r = None if acc is None else acc[k][0]
        total_i = None if acc is None else acc[k][1]
        for j in range(3):
            b = mat(k, j) if adj else mat(j, k)
            a = row[j]
            if adj:
                r = a[0] * b[0] + a[1] * b[1]
                i = a[1] * b[0] - a[0] * b[1]
            else:
                r = a[0] * b[0] - a[1] * b[1]
                i = a[0] * b[1] + a[1] * b[0]
            total_r = r if total_r is None else total_r + r
            total_i = i if total_i is None else total_i + i
        out.append((total_r, total_i))
    return out


def getter(load):
    return lambda i, j: (load(re(i, j)), load(re(i, j) + 1))


def row_of(mat, i):
    return [mat(i, j) for j in range(3)]


def adj_row(mat, i):
    return [conj(mat(j, i)) for j in range(3)]


def full(mat):
    values = [[mat(i, j) for j in range(3)] for i in range(3)]
    return lambda i, j: values[i][j]


def of_rows(rows):
    return lambda i, j: rows[i][j]


def traceless_anti(mat):
    diag = [mat(i, i)[1] for i in range(3)]
    third = (diag[0] + diag[1] + diag[2]) * (1.0 / 3.0)
    diag = [v - third for v in diag]
    zero = jnp.zeros_like(third)
    rows = [[None] * 3 for _ in range(3)]
    for i in range(3):
        rows[i][i] = (zero, diag[i])
        for j in range(i + 1, 3):
            a, b = mat(i, j), mat(j, i)
            up = (0.5 * (a[0] - b[0]), 0.5 * (a[1] + b[1]))
            rows[i][j] = up
            rows[j][i] = (-up[0], up[1])
    return of_rows(rows)


def alg_values(mat):
    out = [mat(0, 0)[1], mat(1, 1)[1]]
    for i, j in ((0, 1), (0, 2), (1, 2)):
        out += list(mat(i, j))
    return out


def alg_matrix(load):
    v = [load(k) for k in range(ALG)]
    zero = jnp.zeros_like(v[0])
    rows = [[None] * 3 for _ in range(3)]
    rows[0][0], rows[1][1], rows[2][2] = (zero, v[0]), (zero, v[1]), (zero, -(v[0] + v[1]))
    for k, (i, j) in enumerate(((0, 1), (0, 2), (1, 2))):
        up = (v[2 + 2 * k], v[3 + 2 * k])
        rows[i][j] = up
        rows[j][i] = (-up[0], up[1])
    return of_rows(rows)


def third_row(load, store):
    g = getter(load)
    a, b = row_of(g, 0), row_of(g, 1)
    for k in range(3):
        p, q = (k + 1) % 3, (k + 2) % 3
        u, v = cmul(a[p], b[q]), cmul(a[q], b[p])
        store(re(2, k), u[0] - v[0])
        store(re(2, k) + 1, v[1] - u[1])


def kernel(
    sizes, links, inc, out,
    own, plus, minus, diag, gown, gplus, gminus, gdiag,
    sig, cst, lam,
    hxm, hxp, hym, hyp, cxy, cyx,
    bx5s, bx0s, by5s, by0s, bx5, bx0, by5, by0,
    yup, ydn, lyup, lydn,
    lxm, lxp, lym, lyp, lcxy, lcyx,
    gxm, gxp, gym, gyp, gcxy, gcyx,
    send_sem, recv_sem,
):
    nx, ny = sizes
    wx, wy = links.shape[2], links.shape[3]
    ts = links.shape[4] - 2
    rows, lanes = wy * ts, links.shape[5]
    mx, my = lax.axis_index("gx"), lax.axis_index("gy")
    xu, xd = lax.rem(mx + 1, nx), lax.rem(mx + nx - 1, nx)
    yu, yd = lax.rem(my + 1, ny), lax.rem(my + ny - 1, ny)
    peers = ((xu, my), (xd, my), (mx, yu), (mx, yd), (xu, yd), (xd, yu))

    barrier = pltpu.get_barrier_semaphore()
    for peer in peers:
        pl.semaphore_signal(barrier, inc=1, device_id=peer, device_id_type=MESH)

    row_id = lax.broadcasted_iota(jnp.int32, (rows, lanes), 0)
    t_id = lax.rem(row_id, ts)

    def sub(v, shift):
        shift = shift % rows
        return v if shift == 0 else pltpu.roll(v, shift, 0)

    def lane(v, shift):
        return pltpu.roll(v, shift % lanes, 1)

    def compact(c, _):
        for d in range(4):
            for x in range(wx):
                for y in range(wy):
                    own[d, c, x, y * ts:(y + 1) * ts, :] = links[d, c, x, y, 1:1 + ts, :]
        return 0

    def pack(c, _):
        for d in range(4):
            for x in range(wx):
                yup[YSLOT[d], c, x * ts:(x + 1) * ts, :] = links[d, c, x, wy - 1, 1:1 + ts, :]
                ydn[YSLOT[d], c, x * ts:(x + 1) * ts, :] = links[d, c, x, 0, 1:1 + ts, :]
        for y in range(wy):
            bx5s[c, y:y + 1, :] = links[AXX, c, wx - 1, y, ts + 1:ts + 2, :]
            bx0s[c, y:y + 1, :] = links[AXT, c, 0, y, 0:1, :]
        for x in range(wx):
            by5s[c, x:x + 1, :] = links[AXY, c, x, wy - 1, ts + 1:ts + 2, :]
            by0s[c, x:x + 1, :] = links[AXT, c, x, 0, 0:1, :]
        return 0

    lax.fori_loop(0, COMP, compact, 0)
    lax.fori_loop(0, SENT, pack, 0)
    pl.semaphore_wait(barrier, len(peers))

    def exchange(items, base):
        copies = []
        for k, (src, dst, peer) in enumerate(items):
            copy = pltpu.make_async_remote_copy(
                src_ref=src, dst_ref=dst, send_sem=send_sem.at[base + k],
                recv_sem=recv_sem.at[base + k], device_id=peer, device_id_type=MESH)
            copy.start()
            copies.append(copy)
        return copies

    s = pl.ds(0, SENT)
    first = exchange((
        (own.at[:, s, wx - 1], hxm.at[:, s], peers[0]),
        (own.at[1:4, s, 0], hxp.at[1:4, s], peers[1]),
        (yup, hym.at[:, s], peers[2]),
        (ydn.at[1:4], hyp.at[1:4, s], peers[3]),
        (own.at[AXX, s, wx - 1], cxy.at[s], peers[4]),
        (own.at[AXY, s, 0], cyx.at[s], peers[5]),
        (bx5s, bx5.at[s], peers[0]),
        (bx0s, bx0.at[s], peers[1]),
        (by5s, by5.at[s], peers[2]),
        (by0s, by0.at[s], peers[3]),
    ), 0)

    def compact_in(c, _):
        for d in range(4):
            for x in range(wx):
                for y in range(wy):
                    sig[d, c, x, y * ts:(y + 1) * ts, :] = inc[d, c, x, y]
        return 0

    lax.fori_loop(0, COMP, compact_in, 0)
    for copy in first:
        copy.wait()

    def fix(ref, *index):
        def store(c, v):
            ref[(*index, c)] = v
        third_row(lambda c: ref[(*index, c)], store)

    def fix_four(d, _):
        fix(hxm, d)
        fix(hym, d)
        return 0

    def fix_three(d, _):
        fix(hxp, d)
        fix(hyp, d)
        return 0

    lax.fori_loop(0, 4, fix_four, 0)
    lax.fori_loop(1, 4, fix_three, 0)
    for ref in (cxy, cyx, bx5, bx0, by5, by0):
        fix(ref)

    def spread(parts):
        v = jnp.broadcast_to(parts[-1], (rows, lanes))
        for y in range(wy - 2, -1, -1):
            v = jnp.where(row_id < (y + 1) * ts, jnp.broadcast_to(parts[y], (rows, lanes)), v)
        return v

    def t_ahead(v, parts):
        edge = 0.0 if parts is None else spread(parts)
        return jnp.where(t_id == ts - 1, edge, sub(v, -1))

    def t_behind(v, parts):
        edge = 0.0 if parts is None else spread(parts)
        return jnp.where(t_id == 0, edge, sub(v, 1))

    def y_ahead(v, halo, x):
        return jnp.where(row_id >= (wy - 1) * ts, sub(halo, (wy - 1 - x) * ts), sub(v, -ts))

    def y_behind(v, halo, x):
        return jnp.where(row_id < ts, sub(halo, -x * ts), sub(v, ts))

    def build(own, plus, minus, diag, hxm, hxp, hym, hyp, cxy, cyx, edges):
        def low(d, c, x):
            return [links[d, c, x, y, 0:1, :] for y in range(wy)] if edges else None

        def high(d, c, x):
            return [links[d, c, x, y, ts + 1:ts + 2, :] for y in range(wy)] if edges else None

        def pick(ref, c, n):
            return [ref[c, k:k + 1, :] for k in range(n)] if edges else None

        def body(c, _):
            for x in range(wx):
                for d in range(4):
                    here = own[d, c, x]
                    if d != AXX:
                        plus[d, AXX, c, x] = own[d, c, x + 1] if x + 1 < wx else hxp[d, c]
                    if d != AXY:
                        plus[d, AXY, c, x] = y_ahead(here, hyp[YSLOT[d], c], x)
                    if d != AXZ:
                        plus[d, AXZ, c, x] = lane(here, -1)
                    if d != AXT:
                        plus[d, AXT, c, x] = t_ahead(here, high(d, c, x))
                    minus[d, AXX, c, x] = own[d, c, x - 1] if x > 0 else hxm[d, c]
                    minus[d, AXY, c, x] = y_behind(here, hym[YSLOT[d], c], x)
                    minus[d, AXZ, c, x] = lane(here, 1)
                    minus[d, AXT, c, x] = t_behind(here, low(d, c, x))
            for x in range(wx):
                last = x + 1 == wx
                if x == 0:
                    edge = hxm[AXX, c]
                    diag[AXX, AXY, c, x] = jnp.where(
                        row_id >= (wy - 1) * ts, sub(cxy[c], (wy - 1) * ts), sub(edge, -ts))
                    diag[AXX, AXZ, c, x] = lane(edge, -1)
                    diag[AXX, AXT, c, x] = t_ahead(edge, pick(bx5, c, wy))
                else:
                    for m in (AXY, AXZ, AXT):
                        diag[AXX, m, c, x] = plus[AXX, m, c, x - 1]
                back = minus[AXY, AXY, c, x]
                if last:
                    diag[AXY, AXX, c, x] = jnp.where(
                        row_id < ts, sub(cyx[c], -(wy - 1) * ts), sub(hxp[AXY, c], ts))
                else:
                    diag[AXY, AXX, c, x] = minus[AXY, AXY, c, x + 1]
                diag[AXY, AXZ, c, x] = lane(back, -1)
                parts = None
                if edges:
                    parts = [by5[c, x:x + 1, :]] + high(AXY, c, x)[:wy - 1]
                diag[AXY, AXT, c, x] = t_ahead(back, parts)
                diag[AXZ, AXX, c, x] = lane(hxp[AXZ, c], 1) if last else minus[AXZ, AXZ, c, x + 1]
                diag[AXZ, AXY, c, x] = lane(plus[AXZ, AXY, c, x], 1)
                diag[AXZ, AXT, c, x] = lane(plus[AXZ, AXT, c, x], 1)
                if last:
                    diag[AXT, AXX, c, x] = t_behind(hxp[AXT, c], pick(bx0, c, wy))
                else:
                    diag[AXT, AXX, c, x] = minus[AXT, AXT, c, x + 1]
                parts = None
                if edges:
                    parts = low(AXT, c, x)[1:] + [by0[c, x:x + 1, :]]
                diag[AXT, AXY, c, x] = t_behind(plus[AXT, AXY, c, x], parts)
                diag[AXT, AXZ, c, x] = lane(minus[AXT, AXT, c, x], -1)
            return 0

        lax.fori_loop(0, COMP, body, 0)

    build(own, plus, minus, diag, hxm, hxp, hym, hyp, cxy, cyx, True)

    def link(ref, *index):
        return getter(lambda c: ref[(*index[:-1], c, index[-1])])

    def site(q, _):
        m, x = q // wx, lax.rem(q, wx)
        c_rows = [None] * 3
        for k in range(1, 4):
            n = lax.rem(m + k, 4)
            n_own, m_ahead, n_ahead = link(own, n, x), link(plus, m, n, x), link(plus, n, m, x)
            n_back, m_back, n_diag = link(minus, n, n, x), link(minus, m, n, x), link(diag, n, m, x)
            for i in range(3):
                part = row_times(row_of(n_own, i), m_ahead)
                c_rows[i] = row_times(part, n_ahead, adj=True, acc=c_rows[i])
                part = row_times(adj_row(n_back, i), m_back)
                c_rows[i] = row_times(part, n_diag, acc=c_rows[i])
        for i in range(3):
            for j in range(3):
                v = c_rows[i][j]
                cst[m, re(i, j), x] = smear_weight * v[0]
                cst[m, re(i, j) + 1, x] = smear_weight * v[1]
        return 0

    lax.fori_loop(0, 4 * wx, site, 0)

    def algebra(q, _):
        m, x = q // wx, lax.rem(q, wx)
        u, staple, target = link(own, m, x), link(cst, m, x), link(sig, m, x)
        omega = of_rows([row_times(row_of(staple, i), u, adj=True) for i in range(3)])
        a = traceless_anti(omega)
        a2 = of_rows([row_times(row_of(a, i), a) for i in range(3)])
        p = 0.5 * (a2(0, 0)[0] + a2(1, 1)[0] + a2(2, 2)[0])
        det = None
        for i in range(3):
            for j in range(3):
                v = cmul(a2(i, j), a(j, i))[1]
                det = v if det is None else det + v
        det = det * (1.0 / 3.0)
        f0 = (1.0 - det * det * (1.0 / 720), det * (1.0 / 6 + p * (1.0 / 120)))
        f1 = (1.0 + p * (1.0 / 6 + p * (1.0 / 120)), det * (1.0 / 24 + p * (1.0 / 360)))
        f2 = (0.5 + p * (1.0 / 24 + p * (1.0 / 720)), det * (1.0 / 120))
        e = []
        for i in range(3):
            e.append([])
            for j in range(3):
                v = cadd(cmul(f1, a(i, j)), cmul(f2, a2(i, j)))
                e[i].append(cadd(v, f0) if i == j else v)
        e = of_rows(e)
        direct = [row_times(adj_row(e, i), target) for i in range(3)]
        cot = of_rows([row_times(row_of(target, i), u, adj=True) for i in range(3)])
        t0 = (cot(0, 0)[0] + cot(1, 1)[0] + cot(2, 2)[0], -(cot(0, 0)[1] + cot(1, 1)[1] + cot(2, 2)[1]))
        t1, t2 = None, None
        for i in range(3):
            for j in range(3):
                g = conj(cot(i, j))
                v1, v2 = cmul(g, a(i, j)), cmul(g, a2(i, j))
                t1 = v1 if t1 is None else cadd(t1, v1)
                t2 = v2 if t2 is None else cadd(t2, v2)
        p_bar = (-t0[1] * det * (1.0 / 120) + t1[0] * (1.0 / 6 + p * (1.0 / 60))
                 - t1[1] * det * (1.0 / 360) + t2[0] * (1.0 / 24 + p * (1.0 / 360)))
        d_bar = (-t0[0] * det * (1.0 / 360) - t0[1] * (1.0 / 6 + p * (1.0 / 120))
                 - t1[1] * (1.0 / 24 + p * (1.0 / 360)) - t2[1] * (1.0 / 120))
        both = []
        for i in range(3):
            v = row_times(row_of(a, i), cot)
            both.append(row_times(row_of(cot, i), a, acc=v))
        bar = []
        g1, g2 = conj(f1), conj(f2)
        for i in range(3):
            bar.append([])
            for j in range(3):
                v1, v2 = cmul(g1, cot(i, j)), cmul(g2, both[i][j])
                aa, aq = a(i, j), a2(i, j)
                bar[i].append((v1[0] - v2[0] - p_bar * aa[0] - d_bar * aq[1],
                               v1[1] - v2[1] - p_bar * aa[1] + d_bar * aq[0]))
        alg = traceless_anti(of_rows(bar))
        for k, v in enumerate(alg_values(alg)):
            lam[m, k, x] = v
        less = [row_times(row_of(alg, i), staple) for i in range(3)]
        for i in range(3):
            for j in range(3):
                cst[m, re(i, j), x] = direct[i][j][0] - less[i][j][0]
                cst[m, re(i, j) + 1, x] = direct[i][j][1] - less[i][j][1]
        return 0

    lax.fori_loop(0, 4 * wx, algebra, 0)

    def pack_alg(k, _):
        for d in range(4):
            for x in range(wx):
                v = lam[d, k, x]
                lyup[YSLOT[d], k, x * ts:(x + 1) * ts, :] = v[(wy - 1) * ts:, :]
                lydn[YSLOT[d], k, x * ts:(x + 1) * ts, :] = v[:ts, :]
        return 0

    lax.fori_loop(0, ALG, pack_alg, 0)
    second = exchange((
        (lam.at[:, :, wx - 1], lxm, peers[0]),
        (lam.at[1:4, :, 0], lxp.at[1:4], peers[1]),
        (lyup, lym, peers[2]),
        (lydn.at[1:4], lyp.at[1:4], peers[3]),
        (lam.at[AXX, :, wx - 1], lcxy, peers[4]),
        (lam.at[AXY, :, 0], lcyx, peers[5]),
    ), len(first))

    def widen(load_alg, load_link, store):
        alg = alg_matrix(lambda k: smear_weight * load_alg(k))
        u = getter(load_link)
        for i in range(3):
            v = row_times(row_of(alg, i), u)
            for j in range(3):
                store(re(i, j), v[j][0])
                store(re(i, j) + 1, v[j][1])

    def widen_own(q, _):
        m, x = q // wx, lax.rem(q, wx)

        def store(c, v):
            gown[m, c, x] = v
        widen(lambda k: lam[m, k, x], lambda c: own[m, c, x], store)
        return 0

    lax.fori_loop(0, 4 * wx, widen_own, 0)
    for copy in second:
        copy.wait()

    def widen_halo(alg, ref, dst, *index):
        def store(c, v):
            dst[(*index, c)] = v
        widen(lambda k: alg[(*index, k)], lambda c: ref[(*index, c)], store)

    def widen_four(d, _):
        widen_halo(lxm, hxm, gxm, d)
        widen_halo(lym, hym, gym, d)
        return 0

    def widen_three(d, _):
        widen_halo(lxp, hxp, gxp, d)
        widen_halo(lyp, hyp, gyp, d)
        return 0

    lax.fori_loop(0, 4, widen_four, 0)
    lax.fori_loop(1, 4, widen_three, 0)
    widen_halo(lcxy, cxy, gcxy)
    widen_halo(lcyx, cyx, gcyx)

    build(gown, gplus, gminus, gdiag, gxm, gxp, gym, gyp, gcxy, gcyx, False)

    def force(q, _):
        m, x = q // wx, lax.rem(q, wx)
        base = link(cst, m, x)
        rows_out = [row_of(base, i) for i in range(3)]
        for k in range(1, 4):
            n = lax.rem(m + k, 4)
            n_own, m_ahead, n_ahead = link(own, n, x), link(plus, m, n, x), link(plus, n, m, x)
            n_back, m_back, n_diag = link(minus, n, n, x), link(minus, m, n, x), link(diag, n, m, x)
            gn_own, gm_ahead, gn_ahead = link(gown, n, x), link(gplus, m, n, x), link(gplus, n, m, x)
            gn_back, gm_back, gn_diag = link(gminus, n, n, x), link(gminus, m, n, x), link(gdiag, n, m, x)
            for i in range(3):
                u_row = row_of(n_own, i)
                v = row_times(u_row, gm_ahead)
                v = row_times(row_of(gn_own, i), m_ahead, acc=v)
                acc = row_times(v, n_ahead, adj=True, acc=rows_out[i])
                v = row_times(u_row, m_ahead)
                acc = row_times(v, gn_ahead, adj=True, acc=acc)
                u_row = adj_row(n_back, i)
                v = row_times(u_row, gm_back)
                v = row_times(adj_row(gn_back, i), m_back, acc=v)
                acc = row_times(v, n_diag, acc=acc)
                v = row_times(u_row, m_back)
                rows_out[i] = row_times(v, gn_diag, acc=acc)
        for i in range(3):
            for j in range(3):
                for part in range(2):
                    v = rows_out[i][j][part]
                    for y in range(wy):
                        out[m, re(i, j) + part, x, y] = v[y * ts:(y + 1) * ts, :]
        return 0

    lax.fori_loop(0, 4 * wx, force, 0)


def solution(mesh):
    sizes = (mesh.shape["gx"], mesh.shape["gy"])

    def body(links, incoming):
        dirs, _, _, _, wx, wy, _, lanes = links.shape
        ts = incoming.shape[6]
        rows = wy * ts
        flat = links.reshape(dirs, COMP, *links.shape[4:])
        flat_in = incoming.reshape(dirs, COMP, *incoming.shape[4:])
        f32 = jnp.float32

        def vm(*shape):
            return pltpu.VMEM((*shape, lanes), f32)

        field = vm(dirs, COMP, wx, rows)
        pairs = vm(dirs, dirs, COMP, wx, rows)
        halo = vm(dirs, COMP, rows)
        corner = vm(COMP, rows)
        scratch = [field, pairs, pairs, pairs, field, pairs, pairs, pairs]
        scratch += [field, field, vm(dirs, ALG, wx, rows)]
        scratch += [halo] * 4 + [corner] * 2
        scratch += [vm(SENT, wy)] * 2 + [vm(SENT, wx)] * 2 + [vm(COMP, wy)] * 2 + [vm(COMP, wx)] * 2
        scratch += [vm(dirs, SENT, rows)] * 2 + [vm(dirs, ALG, rows)] * 2
        scratch += [vm(dirs, ALG, rows)] * 4 + [vm(ALG, rows)] * 2
        scratch += [halo] * 4 + [corner] * 2
        scratch += [pltpu.SemaphoreType.DMA((16,)), pltpu.SemaphoreType.DMA((16,))]
        result = pl.pallas_call(
            partial(kernel, sizes),
            out_shape=jax.ShapeDtypeStruct(flat_in.shape, f32),
            in_specs=[pl.BlockSpec(memory_space=pltpu.VMEM)] * 2,
            out_specs=pl.BlockSpec(memory_space=pltpu.VMEM),
            scratch_shapes=scratch,
            compiler_params=pltpu.CompilerParams(
                collective_id=0, has_side_effects=True, vmem_limit_bytes=60 << 20),
            name="stout",
        )(flat, flat_in)
        return result.reshape(incoming.shape)

    placed = P(None, None, None, None, "gx", "gy", None, None)
    return jax.shard_map(
        body, mesh=mesh, in_specs=(placed, placed), out_specs=placed, check_vma=False)
```

```python
from functools import partial

import jax
import jax.numpy as jnp
from jax import lax
from jax.experimental import pallas as pl
from jax.experimental.pallas import tpu as pltpu
from jax.sharding import PartitionSpec as P

smear_weight = 0.2
MESH = pl.DeviceIdType.MESH
AXX, AXY, AXZ, AXT = 0, 1, 2, 3
SENT = 12
COMP = 18
ALG = 8
YSLOT = (1, 0, 2, 3)


def re(i, j):
    return (i * 3 + j) * 2


def cmul(a, b):
    return (a[0] * b[0] - a[1] * b[1], a[0] * b[1] + a[1] * b[0])


def cadd(a, b):
    return (a[0] + b[0], a[1] + b[1])


def conj(a):
    return (a[0], -a[1])


def row_times(row, mat, adj=False, acc=None):
    out = []
    for k in range(3):
        total_r = None if acc is None else acc[k][0]
        total_i = None if acc is None else acc[k][1]
        for j in range(3):
            b = mat(k, j) if adj else mat(j, k)
            a = row[j]
            if adj:
                r = a[0] * b[0] + a[1] * b[1]
                i = a[1] * b[0] - a[0] * b[1]
            else:
                r = a[0] * b[0] - a[1] * b[1]
                i = a[0] * b[1] + a[1] * b[0]
            total_r = r if total_r is None else total_r + r
            total_i = i if total_i is None else total_i + i
        out.append((total_r, total_i))
    return out


def getter(load):
    return lambda i, j: (load(re(i, j)), load(re(i, j) + 1))


def row_of(mat, i):
    return [mat(i, j) for j in range(3)]


def adj_row(mat, i):
    return [conj(mat(j, i)) for j in range(3)]


def full(mat):
    values = [[mat(i, j) for j in range(3)] for i in range(3)]
    return lambda i, j: values[i][j]


def of_rows(rows):
    return lambda i, j: rows[i][j]


def traceless_anti(mat):
    diag = [mat(i, i)[1] for i in range(3)]
    third = (diag[0] + diag[1] + diag[2]) * (1.0 / 3.0)
    diag = [v - third for v in diag]
    zero = jnp.zeros_like(third)
    rows = [[None] * 3 for _ in range(3)]
    for i in range(3):
        rows[i][i] = (zero, diag[i])
        for j in range(i + 1, 3):
            a, b = mat(i, j), mat(j, i)
            up = (0.5 * (a[0] - b[0]), 0.5 * (a[1] + b[1]))
            rows[i][j] = up
            rows[j][i] = (-up[0], up[1])
    return of_rows(rows)


def alg_values(mat):
    out = [mat(0, 0)[1], mat(1, 1)[1]]
    for i, j in ((0, 1), (0, 2), (1, 2)):
        out += list(mat(i, j))
    return out


def alg_matrix(load):
    v = [load(k) for k in range(ALG)]
    zero = jnp.zeros_like(v[0])
    rows = [[None] * 3 for _ in range(3)]
    rows[0][0], rows[1][1], rows[2][2] = (zero, v[0]), (zero, v[1]), (zero, -(v[0] + v[1]))
    for k, (i, j) in enumerate(((0, 1), (0, 2), (1, 2))):
        up = (v[2 + 2 * k], v[3 + 2 * k])
        rows[i][j] = up
        rows[j][i] = (-up[0], up[1])
    return of_rows(rows)


def third_row(load, store):
    g = getter(load)
    a, b = row_of(g, 0), row_of(g, 1)
    for k in range(3):
        p, q = (k + 1) % 3, (k + 2) % 3
        u, v = cmul(a[p], b[q]), cmul(a[q], b[p])
        store(re(2, k), u[0] - v[0])
        store(re(2, k) + 1, v[1] - u[1])


def kernel(
    sizes, links, inc, out,
    own, plus, minus, diag, gown, gplus, gminus, gdiag,
    sig, cst, lam,
    hxm, hxp, hym, hyp, cxy, cyx,
    cxs, cys, lcxs, lcys, bx5s, bx0s, by5s, by0s, bx5, bx0, by5, by0,
    yup, ydn, lyup, lydn,
    lxm, lxp, lym, lyp, lcxy, lcyx,
    gxm, gxp, gym, gyp, gcxy, gcyx,
    send_sem, recv_sem,
):
    nx, ny = sizes
    wx, wy = links.shape[2], links.shape[3]
    ts = links.shape[4] - 2
    rows, lanes = wy * ts, links.shape[5]
    mx, my = lax.axis_index("gx"), lax.axis_index("gy")
    xu, xd = lax.rem(mx + 1, nx), lax.rem(mx + nx - 1, nx)
    yu, yd = lax.rem(my + 1, ny), lax.rem(my + ny - 1, ny)
    peers = ((xu, my), (xd, my), (mx, yu), (mx, yd), (xu, yd), (xd, yu))

    barrier = pltpu.get_barrier_semaphore()
    for peer in peers:
        pl.semaphore_signal(barrier, inc=1, device_id=peer, device_id_type=MESH)

    row_id = lax.broadcasted_iota(jnp.int32, (rows, lanes), 0)
    t_id = lax.rem(row_id, ts)

    def sub(v, shift):
        shift = shift % rows
        return v if shift == 0 else pltpu.roll(v, shift, 0)

    def lane(v, shift):
        return pltpu.roll(v, shift % lanes, 1)

    def tiled(v):
        return jnp.concatenate([v] * wy, axis=0)

    def compact(c, _):
        for d in range(4):
            for x in range(wx):
                for y in range(wy):
                    own[d, c, x, y * ts:(y + 1) * ts, :] = links[d, c, x, y, 1:1 + ts, :]
        return 0

    def pack(c, _):
        for d in range(4):
            for x in range(wx):
                yup[YSLOT[d], c, x * ts:(x + 1) * ts, :] = links[d, c, x, wy - 1, 1:1 + ts, :]
                ydn[YSLOT[d], c, x * ts:(x + 1) * ts, :] = links[d, c, x, 0, 1:1 + ts, :]
        cxs[c] = links[AXX, c, wx - 1, 0, 1:1 + ts, :]
        cys[c] = links[AXY, c, 0, wy - 1, 1:1 + ts, :]
        for y in range(wy):
            bx5s[c, y:y + 1, :] = links[AXX, c, wx - 1, y, ts + 1:ts + 2, :]
            bx0s[c, y:y + 1, :] = links[AXT, c, 0, y, 0:1, :]
        for x in range(wx):
            by5s[c, x:x + 1, :] = links[AXY, c, x, wy - 1, ts + 1:ts + 2, :]
            by0s[c, x:x + 1, :] = links[AXT, c, x, 0, 0:1, :]
        return 0

    lax.fori_loop(0, COMP, compact, 0)
    lax.fori_loop(0, SENT, pack, 0)
    pl.semaphore_wait(barrier, len(peers))

    def exchange(items, base):
        copies = []
        for k, (src, dst, peer) in enumerate(items):
            copy = pltpu.make_async_remote_copy(
                src_ref=src, dst_ref=dst, send_sem=send_sem.at[base + k],
                recv_sem=recv_sem.at[base + k], device_id=peer, device_id_type=MESH)
            copy.start()
            copies.append(copy)
        return copies

    s = pl.ds(0, SENT)
    first = exchange((
        (own.at[:, s, wx - 1], hxm.at[:, s], peers[0]),
        (own.at[1:4, s, 0], hxp.at[1:4, s], peers[1]),
        (yup, hym.at[:, s], peers[2]),
        (ydn.at[1:4], hyp.at[1:4, s], peers[3]),
        (cxs, cxy.at[s], peers[4]),
        (cys, cyx.at[s], peers[5]),
        (bx5s, bx5.at[s], peers[0]),
        (bx0s, bx0.at[s], peers[1]),
        (by5s, by5.at[s], peers[2]),
        (by0s, by0.at[s], peers[3]),
    ), 0)

    def compact_in(c, _):
        for d in range(4):
            for x in range(wx):
                for y in range(wy):
                    sig[d, c, x, y * ts:(y + 1) * ts, :] = inc[d, c, x, y]
                cst[d, c, x] = jnp.zeros((rows, lanes), jnp.float32)
        return 0

    lax.fori_loop(0, COMP, compact_in, 0)
    def fix(ref, *index):
        def store(c, v):
            ref[(*index, c)] = v
        third_row(lambda c: ref[(*index, c)], store)

    def fix_y():
        def four(d, _):
            fix(hym, d)
            return 0

        def three(d, _):
            fix(hyp, d)
            return 0

        lax.fori_loop(0, 4, four, 0)
        lax.fori_loop(1, 4, three, 0)
        for ref in (by5, by0):
            fix(ref)

    def fix_x():
        def four(d, _):
            fix(hxm, d)
            return 0

        def three(d, _):
            fix(hxp, d)
            return 0

        lax.fori_loop(0, 4, four, 0)
        lax.fori_loop(1, 4, three, 0)
        for ref in (cxy, cyx, bx5, bx0):
            fix(ref)

    def spread(parts):
        v = jnp.broadcast_to(parts[-1], (rows, lanes))
        for y in range(wy - 2, -1, -1):
            v = jnp.where(row_id < (y + 1) * ts, jnp.broadcast_to(parts[y], (rows, lanes)), v)
        return v

    def t_ahead(v, parts):
        edge = 0.0 if parts is None else spread(parts)
        return jnp.where(t_id == ts - 1, edge, sub(v, -1))

    def t_behind(v, parts):
        edge = 0.0 if parts is None else spread(parts)
        return jnp.where(t_id == 0, edge, sub(v, 1))

    def y_ahead(v, halo, x):
        return jnp.where(row_id >= (wy - 1) * ts, sub(halo, (wy - 1 - x) * ts), sub(v, -ts))

    def y_behind(v, halo, x):
        return jnp.where(row_id < ts, sub(halo, -x * ts), sub(v, ts))

    def build(own, plus, minus, diag, hxm, hxp, hym, hyp, cxy, cyx, edges, stage):
        def low(d, c, x):
            return [links[d, c, x, y, 0:1, :] for y in range(wy)] if edges else None

        def high(d, c, x):
            return [links[d, c, x, y, ts + 1:ts + 2, :] for y in range(wy)] if edges else None

        def pick(ref, c, n):
            return [ref[c, k:k + 1, :] for k in range(n)] if edges else None

        def body(c, _):
            for x in range(wx):
                for d in range(4):
                    here = own[d, c, x]
                    if stage == 0:
                        if d != AXX:
                            plus[d, AXX, c, x] = own[d, c, x + 1] if x + 1 < wx else hxp[d, c]
                        minus[d, AXX, c, x] = own[d, c, x - 1] if x > 0 else hxm[d, c]
                    if stage == 1:
                        if d != AXY:
                            plus[d, AXY, c, x] = y_ahead(here, hyp[YSLOT[d], c], x)
                        minus[d, AXY, c, x] = y_behind(here, hym[YSLOT[d], c], x)
                    if stage == 2:
                        if d != AXZ:
                            plus[d, AXZ, c, x] = lane(here, -1)
                        if d != AXT:
                            plus[d, AXT, c, x] = t_ahead(here, high(d, c, x))
                        minus[d, AXZ, c, x] = lane(here, 1)
                        minus[d, AXT, c, x] = t_behind(here, low(d, c, x))
            for x in range(wx):
                last = x + 1 == wx
                if stage == 2:
                    diag[AXZ, AXT, c, x] = lane(plus[AXZ, AXT, c, x], 1)
                    diag[AXT, AXZ, c, x] = lane(minus[AXT, AXT, c, x], -1)
                if stage == 1:
                    back = minus[AXY, AXY, c, x]
                    diag[AXY, AXZ, c, x] = lane(back, -1)
                    parts = None
                    if edges:
                        parts = [by5[c, x:x + 1, :]] + high(AXY, c, x)[:wy - 1]
                    diag[AXY, AXT, c, x] = t_ahead(back, parts)
                    diag[AXZ, AXY, c, x] = lane(plus[AXZ, AXY, c, x], 1)
                    parts = None
                    if edges:
                        parts = low(AXT, c, x)[1:] + [by0[c, x:x + 1, :]]
                    diag[AXT, AXY, c, x] = t_behind(plus[AXT, AXY, c, x], parts)
                if stage == 0:
                    if x == 0:
                        edge = hxm[AXX, c]
                        diag[AXX, AXY, c, x] = jnp.where(
                            row_id >= (wy - 1) * ts, tiled(cxy[c]), sub(edge, -ts))
                        diag[AXX, AXZ, c, x] = lane(edge, -1)
                        diag[AXX, AXT, c, x] = t_ahead(edge, pick(bx5, c, wy))
                    else:
                        for m in (AXY, AXZ, AXT):
                            diag[AXX, m, c, x] = plus[AXX, m, c, x - 1]
                    if last:
                        diag[AXY, AXX, c, x] = jnp.where(
                            row_id < ts, tiled(cyx[c]), sub(hxp[AXY, c], ts))
                        diag[AXZ, AXX, c, x] = lane(hxp[AXZ, c], 1)
                        diag[AXT, AXX, c, x] = t_behind(hxp[AXT, c], pick(bx0, c, wy))
                    else:
                        for m in (AXY, AXZ, AXT):
                            diag[m, AXX, c, x] = minus[m, m, c, x + 1]
            return 0

        lax.fori_loop(0, COMP, body, 0)

    def build_links(stage):
        build(own, plus, minus, diag, hxm, hxp, hym, hyp, cxy, cyx, True, stage)

    def link(ref, *index):
        return getter(lambda c: ref[(*index[:-1], c, index[-1])])

    def planes(base, work):
        def step(q, _):
            pair, x = q // wx, lax.rem(q, wx)
            gap, swap = 1 + pair // 2, lax.rem(pair, 2)
            work(base + gap * swap, base + gap * (1 - swap), x)
            return 0

        lax.fori_loop(0, 2 * (3 - base) * wx, step, 0)

    def put(m, x, i, values):
        for j in range(3):
            cst[m, re(i, j), x] = values[j][0]
            cst[m, re(i, j) + 1, x] = values[j][1]

    def site(m, n, x):
        n_own, m_ahead, n_ahead = link(own, n, x), link(plus, m, n, x), link(plus, n, m, x)
        n_back, m_back, n_diag = link(minus, n, n, x), link(minus, m, n, x), link(diag, n, m, x)
        total = link(cst, m, x)
        for i in range(3):
            part = row_times(row_of(n_own, i), m_ahead)
            acc = row_times(part, n_ahead, adj=True, acc=row_of(total, i))
            part = row_times(adj_row(n_back, i), m_back)
            put(m, x, i, row_times(part, n_diag, acc=acc))

    build_links(2)
    planes(2, site)
    for k in (2, 3, 8, 9):
        first[k].wait()
    fix_y()
    build_links(1)
    planes(1, site)
    for k in (0, 1, 4, 5, 6, 7):
        first[k].wait()
    fix_x()
    build_links(0)
    planes(0, site)

    def algebra(m, x, _):
        u, raw, target = link(own, m, x), link(cst, m, x), link(sig, m, x)
        staple = full(lambda i, j: tuple(smear_weight * v for v in raw(i, j)))
        omega = of_rows([row_times(row_of(staple, i), u, adj=True) for i in range(3)])
        a = traceless_anti(omega)
        a2 = of_rows([row_times(row_of(a, i), a) for i in range(3)])
        p = 0.5 * (a2(0, 0)[0] + a2(1, 1)[0] + a2(2, 2)[0])
        det = None
        for i in range(3):
            for j in range(3):
                v = cmul(a2(i, j), a(j, i))[1]
                det = v if det is None else det + v
        det = det * (1.0 / 3.0)
        f0 = (1.0 - det * det * (1.0 / 720), det * (1.0 / 6 + p * (1.0 / 120)))
        f1 = (1.0 + p * (1.0 / 6 + p * (1.0 / 120)), det * (1.0 / 24 + p * (1.0 / 360)))
        f2 = (0.5 + p * (1.0 / 24 + p * (1.0 / 720)), det * (1.0 / 120))
        e = []
        for i in range(3):
            e.append([])
            for j in range(3):
                v = cadd(cmul(f1, a(i, j)), cmul(f2, a2(i, j)))
                e[i].append(cadd(v, f0) if i == j else v)
        e = of_rows(e)
        direct = [row_times(adj_row(e, i), target) for i in range(3)]
        cot = of_rows([row_times(row_of(target, i), u, adj=True) for i in range(3)])
        t0 = (cot(0, 0)[0] + cot(1, 1)[0] + cot(2, 2)[0], -(cot(0, 0)[1] + cot(1, 1)[1] + cot(2, 2)[1]))
        t1, t2 = None, None
        for i in range(3):
            for j in range(3):
                g = conj(cot(i, j))
                v1, v2 = cmul(g, a(i, j)), cmul(g, a2(i, j))
                t1 = v1 if t1 is None else cadd(t1, v1)
                t2 = v2 if t2 is None else cadd(t2, v2)
        p_bar = (-t0[1] * det * (1.0 / 120) + t1[0] * (1.0 / 6 + p * (1.0 / 60))
                 - t1[1] * det * (1.0 / 360) + t2[0] * (1.0 / 24 + p * (1.0 / 360)))
        d_bar = (-t0[0] * det * (1.0 / 360) - t0[1] * (1.0 / 6 + p * (1.0 / 120))
                 - t1[1] * (1.0 / 24 + p * (1.0 / 360)) - t2[1] * (1.0 / 120))
        both = []
        for i in range(3):
            v = row_times(row_of(a, i), cot)
            both.append(row_times(row_of(cot, i), a, acc=v))
        bar = []
        g1, g2 = conj(f1), conj(f2)
        for i in range(3):
            bar.append([])
            for j in range(3):
                v1, v2 = cmul(g1, cot(i, j)), cmul(g2, both[i][j])
                aa, aq = a(i, j), a2(i, j)
                bar[i].append((v1[0] - v2[0] - p_bar * aa[0] - d_bar * aq[1],
                               v1[1] - v2[1] - p_bar * aa[1] + d_bar * aq[0]))
        alg = traceless_anti(of_rows(bar))
        for k, v in enumerate(alg_values(alg)):
            lam[m, k, x] = v
        less = [row_times(row_of(alg, i), staple) for i in range(3)]
        for i in range(3):
            for j in range(3):
                cst[m, re(i, j), x] = direct[i][j][0] - less[i][j][0]
                cst[m, re(i, j) + 1, x] = direct[i][j][1] - less[i][j][1]
        return 0

    second_x, second_y = [], []
    for m in range(4):
        lax.fori_loop(0, wx, partial(algebra, m), 0)
        slot = YSLOT[m]
        for k in range(ALG):
            for x in range(wx):
                v = lam[m, k, x]
                lyup[slot, k, x * ts:(x + 1) * ts, :] = v[(wy - 1) * ts:, :]
                if m != AXY:
                    lydn[slot, k, x * ts:(x + 1) * ts, :] = v[:ts, :]
            if m == AXX:
                lcxs[k] = lam[m, k, wx - 1][:ts, :]
            if m == AXY:
                lcys[k] = lam[m, k, 0][(wy - 1) * ts:, :]
        items = [(lam.at[m, :, wx - 1], lxm.at[m], peers[0])]
        if m != AXX:
            items.append((lam.at[m, :, 0], lxp.at[m], peers[1]))
        if m == AXX:
            items.append((lcxs, lcxy, peers[4]))
        if m == AXY:
            items.append((lcys, lcyx, peers[5]))
        second_x += exchange(items, len(first) + len(second_x) + len(second_y))
        items = [(lyup.at[slot], lym.at[slot], peers[2])]
        if m != AXY:
            items.append((lydn.at[slot], lyp.at[slot], peers[3]))
        second_y += exchange(items, len(first) + len(second_x) + len(second_y))

    def widen(load_alg, load_link, store):
        alg = alg_matrix(lambda k: smear_weight * load_alg(k))
        u = getter(load_link)
        for i in range(3):
            v = row_times(row_of(alg, i), u)
            for j in range(3):
                store(re(i, j), v[j][0])
                store(re(i, j) + 1, v[j][1])

    def widen_own(q, _):
        m, x = q // wx, lax.rem(q, wx)

        def store(c, v):
            gown[m, c, x] = v
        widen(lambda k: lam[m, k, x], lambda c: own[m, c, x], store)
        return 0

    lax.fori_loop(0, 4 * wx, widen_own, 0)
    def widen_halo(alg, ref, dst, *index):
        def store(c, v):
            dst[(*index, c)] = v
        widen(lambda k: alg[(*index, k)], lambda c: ref[(*index, c)], store)

    def widen_faces(pairs_four, pairs_three):
        def four(d, _):
            widen_halo(*pairs_four, d)
            return 0

        def three(d, _):
            widen_halo(*pairs_three, d)
            return 0

        lax.fori_loop(0, 4, four, 0)
        lax.fori_loop(1, 4, three, 0)

    def build_g(stage):
        build(gown, gplus, gminus, gdiag, gxm, gxp, gym, gyp, gcxy, gcyx, False, stage)

    def force(m, n, x):
        n_own, m_ahead, n_ahead = link(own, n, x), link(plus, m, n, x), link(plus, n, m, x)
        n_back, m_back, n_diag = link(minus, n, n, x), link(minus, m, n, x), link(diag, n, m, x)
        gn_own, gm_ahead, gn_ahead = link(gown, n, x), link(gplus, m, n, x), link(gplus, n, m, x)
        gn_back, gm_back, gn_diag = link(gminus, n, n, x), link(gminus, m, n, x), link(gdiag, n, m, x)
        total = link(cst, m, x)
        for i in range(3):
            u_row = row_of(n_own, i)
            v = row_times(u_row, gm_ahead)
            v = row_times(row_of(gn_own, i), m_ahead, acc=v)
            acc = row_times(v, n_ahead, adj=True, acc=row_of(total, i))
            v = row_times(u_row, m_ahead)
            acc = row_times(v, gn_ahead, adj=True, acc=acc)
            u_row = adj_row(n_back, i)
            v = row_times(u_row, gm_back)
            v = row_times(adj_row(gn_back, i), m_back, acc=v)
            acc = row_times(v, n_diag, acc=acc)
            v = row_times(u_row, m_back)
            put(m, x, i, row_times(v, gn_diag, acc=acc))

    build_g(2)
    planes(2, force)
    for copy in second_y:
        copy.wait()
    widen_faces((lym, hym, gym), (lyp, hyp, gyp))
    build_g(1)
    planes(1, force)
    for copy in second_x:
        copy.wait()
    widen_faces((lxm, hxm, gxm), (lxp, hxp, gxp))
    widen_halo(lcxy, cxy, gcxy)
    widen_halo(lcyx, cyx, gcyx)
    build_g(0)
    planes(0, force)

    def deliver(c, _):
        for d in range(4):
            for x in range(wx):
                for y in range(wy):
                    out[d, c, x, y] = cst[d, c, x, y * ts:(y + 1) * ts, :]
        return 0

    lax.fori_loop(0, COMP, deliver, 0)


def solution(mesh):
    sizes = (mesh.shape["gx"], mesh.shape["gy"])

    def body(links, incoming):
        dirs, _, _, _, wx, wy, _, lanes = links.shape
        ts = incoming.shape[6]
        rows = wy * ts
        flat = links.reshape(dirs, COMP, *links.shape[4:])
        flat_in = incoming.reshape(dirs, COMP, *incoming.shape[4:])
        f32 = jnp.float32

        def vm(*shape):
            return pltpu.VMEM((*shape, lanes), f32)

        field = vm(dirs, COMP, wx, rows)
        pairs = vm(dirs, dirs, COMP, wx, rows)
        halo = vm(dirs, COMP, rows)
        corner = vm(COMP, ts)
        scratch = [field, pairs, pairs, pairs, field, pairs, pairs, pairs]
        scratch += [field, field, vm(dirs, ALG, wx, rows)]
        scratch += [halo] * 4 + [corner] * 2
        scratch += [vm(SENT, ts)] * 2 + [vm(ALG, ts)] * 2
        scratch += [vm(SENT, wy)] * 2 + [vm(SENT, wx)] * 2 + [vm(COMP, wy)] * 2 + [vm(COMP, wx)] * 2
        scratch += [vm(dirs, SENT, rows)] * 2 + [vm(dirs, ALG, rows)] * 2
        scratch += [vm(dirs, ALG, rows)] * 4 + [vm(ALG, ts)] * 2
        scratch += [halo] * 4 + [corner] * 2
        scratch += [pltpu.SemaphoreType.DMA((26,)), pltpu.SemaphoreType.DMA((26,))]
        result = pl.pallas_call(
            partial(kernel, sizes),
            out_shape=jax.ShapeDtypeStruct(flat_in.shape, f32),
            in_specs=[pl.BlockSpec(memory_space=pltpu.VMEM)] * 2,
            out_specs=pl.BlockSpec(memory_space=pltpu.VMEM),
            scratch_shapes=scratch,
            compiler_params=pltpu.CompilerParams(
                collective_id=0, has_side_effects=True, vmem_limit_bytes=60 << 20),
            name="stout",
        )(flat, flat_in)
        return result.reshape(incoming.shape)

    placed = P(None, None, None, None, "gx", "gy", None, None)
    return jax.shard_map(
        body, mesh=mesh, in_specs=(placed, placed), out_specs=placed, check_vma=False)
```
